256 devices in a mesh: expert: 16 (over y, x), hidden: 16 (over z, core).
Axes of the slice: x: 4, y: 4, z: 8, core: 2. Of those that a mesh axis runs over, the one named last changes fastest.
Arguments:
- layer_input: bfloat16 [4096, 4096], P('expert', 'hidden'), may hold values from -6 to 6
- output_grad: bfloat16 [4096, 4096], P('expert', 'hidden'), may hold values from -1.5 to 1.5
- latent_saved: bfloat16 [4096, 1024], P('expert'), may hold values from -6 to 6
- combined_saved: bfloat16 [4096, 1024], P('expert'), may hold values from -6 to 6
- expert_ids: int32 [4096, 22], P('expert'), may hold values from 0 to 511, as said below
- gate_values: bfloat16 [4096, 22], P('expert'), may hold values from 0.099609375 to 1.5
- down_proj: bfloat16 [1024, 4096], P(None, 'hidden'), may hold values from -0.09375 to 0.09375
- up_proj: bfloat16 [1024, 4096], P(None, 'hidden'), may hold values from -0.1875 to 0.1875
- expert_in: bfloat16 [16, 1024, 2688], P('expert', None, 'hidden'), may hold values from -0.1875 to 0.1875
- expert_out: bfloat16 [16, 2688, 1024], P('expert', 'hidden'), may hold values from -0.125 to 0.125
Outputs:
- input_grad: bfloat16 [4096, 4096], P('expert', 'hidden')
- down_grad: float32 [1024, 4096], P('expert', 'hidden')
- up_grad: float32 [1024, 4096], P('expert', 'hidden')
- gate_grad: float32 [4096, 22], P('expert')
- expert_in_grad: float32 [16, 1024, 2688], P('expert', None, 'hidden')
- expert_out_grad: float32 [16, 2688, 1024], P('expert', 'hidden')
The draws below stay inside these ranges and needn't reach their ends.
Inputs may be any that keep to these rules, and one draw needn't show every extreme that they name: `expert_ids`: each row names 22 different experts. In each aligned block of 256 rows (the rows of one index of the expert axis) each expert below 16 is named by at most 24 rows; some expert below 16 is named by exactly 24 rows in every block.
All inputs are finite; a program needn't handle non-finite values.
Results may differ from the reference program's by a relative error of at most 0.0065.
Values may be sent and summed in bfloat16 or wider, within the bound.
No kernel may reach another device: no remote copies, remote signals or barrier semaphores. Data moves between devices by JAX's collectives and lax.ppermute only.
A program may use at most 64 MiB of HBM per device.

```python
import math
import jax
import jax.numpy as jnp
from jax import lax

D = 4096
LATENT = 1024
FF = 2688
EXPERTS = 512
TOPK = 22
TOK_DEV = 256
TOKENS = 4096
LIVE = 16
CAP = 24
N_EXPERT = 16


def draw_expert_ids(key, part):
    keys = jax.random.split(key, 8)
    blocks = TOKENS // TOK_DEV
    experts = jnp.arange(LIVE, dtype=jnp.int32)
    popular = jax.random.randint(keys[0], (LIVE,), 1, 5)
    counts = jax.random.randint(keys[1], (blocks, LIVE), 0, CAP + 1) * popular[None, :] // 4
    counts = jnp.minimum(counts, CAP)
    always_full = jax.random.randint(keys[2], (), 0, LIVE)
    extra_full = jax.random.randint(keys[3], (blocks,), 0, LIVE)
    at_limit = (experts[None, :] == always_full) | (experts[None, :] == extra_full[:, None])
    counts = jnp.where(at_limit, CAP, counts).astype(jnp.int32)
    scores = jax.random.randint(keys[4], (blocks, LIVE), 0, LIVE) * LIVE + experts[None, :]
    order = jnp.argsort(scores, axis=1).astype(jnp.int32)
    ordered = jnp.take_along_axis(counts, order, axis=1)
    starts_ordered = jnp.cumsum(ordered, axis=1) - ordered
    inverse = jnp.argsort(order, axis=1).astype(jnp.int32)
    starts = jnp.take_along_axis(starts_ordered, inverse, axis=1)
    token_iota = jnp.arange(TOK_DEV, dtype=jnp.int32)
    token_scores = jax.random.randint(keys[5], (blocks, TOK_DEV), 0, TOK_DEV) * TOK_DEV + token_iota[None, :]
    place = jnp.argsort(token_scores, axis=1).astype(jnp.int32)
    chosen = (jnp.mod(place[:, :, None] - starts[:, None, :], TOK_DEV) < counts[:, None, :]).astype(jnp.int32)
    chosen = chosen.reshape(TOKENS, LIVE)
    many = jnp.sum(chosen, axis=1)
    order_rank = jnp.cumsum(chosen, axis=1) - chosen
    shift_by = jax.random.randint(keys[6], (TOKENS,), 0, TOPK)
    begin_at = jax.random.randint(keys[7], (TOKENS,), 0, EXPERTS - LIVE)
    column = jnp.mod(jnp.arange(TOPK, dtype=jnp.int32)[None, :] - shift_by[:, None], TOPK)
    hit_table = chosen[:, None, :] * (order_rank[:, None, :] == column[:, :, None]).astype(jnp.int32)
    live_pick = jnp.sum(hit_table * experts[None, None, :], axis=2)
    other_pick = LIVE + jnp.mod(begin_at[:, None] + column - many[:, None], EXPERTS - LIVE)
    return jnp.where(column < many[:, None], live_pick, other_pick).astype(jnp.int32)


def levels(own_key, dims, pieces, low, high):
    def one(position, shards_of):
        draws = jax.random.uniform(jax.random.fold_in(jax.random.fold_in(own_key, 6), position), (shards_of,), jnp.float32, low / len(pieces), high / len(pieces))
        return jnp.repeat(jnp.exp(draws), dims[position] // shards_of).reshape((-1,) + (1,) * (len(dims) - position - 1))

    loudness = one(*pieces[0])
    for cut in pieces[1:]:
        loudness = loudness * one(*cut)
    return loudness


def bell_draw(own_key, dims, deviation, reach, shards=(), kind=jnp.bfloat16):
    drawn = jax.random.normal(own_key, dims, jnp.float32) * deviation
    if len(shards) > 0:
        drawn = levels(own_key, dims, shards, -0.22, 0.18) * drawn
    return jnp.clip(drawn, min=-reach, max=reach).astype(kind)


def setup_inputs(seed: int = 0) -> dict:
    key_list = jax.random.split(jax.random.key(seed), 11)
    return {
        "layer_input": bell_draw(key_list[0], (TOKENS, D), 1.0, 6.0, ((0, 16), (1, 16))),
        "output_grad": bell_draw(key_list[1], (TOKENS, D), 0.25, 1.5, ((0, 16), (1, 16))),
        "latent_saved": bell_draw(key_list[2], (TOKENS, LATENT), 1.0, 6.0, ((0, 16),)),
        "combined_saved": bell_draw(key_list[3], (TOKENS, LATENT), 1.0, 6.0, ((0, 16),)),
        "expert_ids": draw_expert_ids(jax.random.fold_in(key_list[10], 71), 0),
        "gate_values": jnp.clip(jnp.exp(math.log(1.5) - 2.7119641 * jax.random.uniform(key_list[5], (TOKENS, TOPK), jnp.float32) ** levels(key_list[5], (TOKENS, TOPK), ((0, 16),), -0.2, 0.2)), 0.099609375, 1.5).astype(jnp.bfloat16),
        "down_proj": bell_draw(key_list[6], (LATENT, D), D ** -0.5, 0.09375, ((1, 16),)),
        "up_proj": bell_draw(key_list[7], (LATENT, D), LATENT ** -0.5, 0.1875, ((1, 16),)),
        "expert_in": bell_draw(key_list[8], (LIVE, LATENT, FF), LATENT ** -0.5, 0.1875, ((0, 16), (2, 16))),
        "expert_out": bell_draw(key_list[9], (LIVE, FF, LATENT), FF ** -0.5, 0.125, ((0, 16), (1, 16))),
    }


def reference(layer_input, output_grad, latent_saved, combined_saved, expert_ids, gate_values, down_proj, up_proj, expert_in, expert_out):
    latent_cot = jnp.dot(output_grad, up_proj.T, preferred_element_type=jnp.float32).astype(jnp.bfloat16)
    up_grad = jnp.dot(combined_saved.T, output_grad, preferred_element_type=jnp.float32)
    gates = gate_values.astype(jnp.float32)
    row_limit = N_EXPERT * CAP

    def expert_step(running, inputs):
        latent_grad, gate_grad = running
        expert, first, second = inputs
        chosen = expert_ids == expert
        routed = jnp.any(chosen, axis=1)
        gate_token = jnp.sum(jnp.where(chosen, gates, jnp.zeros_like(gates)), axis=1)
        row_index = jnp.nonzero(routed, size=row_limit, fill_value=0)[0].astype(jnp.int32)
        filled = (jnp.arange(row_limit, dtype=jnp.int32) < jnp.sum(routed.astype(jnp.int32))).astype(jnp.float32)
        latent_rows = latent_saved[row_index]
        grad_rows = latent_cot[row_index]
        gate_rows = gate_token[row_index] * filled
        pre_act = jnp.dot(latent_rows, first, preferred_element_type=jnp.float32)
        relu_out = jnp.maximum(pre_act, 0.0)
        back_proj = jnp.dot(grad_rows, second.T, preferred_element_type=jnp.float32)
        gate_back = jnp.sum(back_proj * relu_out * relu_out, axis=1) * filled
        scaled_act = (gate_rows[:, None] * relu_out * relu_out).astype(jnp.bfloat16)
        pre_grad = (2.0 * gate_rows[:, None] * relu_out * back_proj).astype(jnp.bfloat16)
        grad_second = jnp.dot(scaled_act.T, grad_rows, preferred_element_type=jnp.float32)
        grad_first = jnp.dot(latent_rows.T, pre_grad, preferred_element_type=jnp.float32)
        latent_back = jnp.dot(pre_grad, first.T, preferred_element_type=jnp.float32)
        latent_grad = latent_grad.at[row_index].add(latent_back * filled[:, None])
        token_gate = jnp.zeros((TOKENS,), jnp.float32).at[row_index].add(gate_back)
        gate_grad = gate_grad + jnp.where(chosen, token_gate[:, None], jnp.zeros_like(gate_grad))
        return (latent_grad, gate_grad), (grad_first, grad_second)

    start = (jnp.zeros((TOKENS, LATENT), jnp.float32), jnp.zeros((TOKENS, TOPK), jnp.float32))
    (latent_grad, gate_grad), (expert_in_grad, expert_out_grad) = lax.scan(
        expert_step, start, (jnp.arange(LIVE, dtype=jnp.int32), expert_in, expert_out))
    latent_bf = latent_grad.astype(jnp.bfloat16)
    input_grad = jnp.dot(latent_bf, down_proj, preferred_element_type=jnp.float32).astype(jnp.bfloat16)
    down_grad = jnp.dot(latent_bf.T, layer_input, preferred_element_type=jnp.float32)
    return input_grad, down_grad, up_grad, gate_grad, expert_in_grad, expert_out_grad
```

```python
import jax
import jax.numpy as jnp
from jax import lax
from jax.sharding import PartitionSpec as P

BF = jnp.bfloat16
F32 = jnp.float32


def mm(a, b, dims):
    return lax.dot_general(a, b, (dims, ((), ())), preferred_element_type=F32)


def on_device(
    layer_input,
    output_grad,
    latent_saved,
    combined_saved,
    expert_ids,
    gate_values,
    down_proj,
    up_proj,
    expert_in,
    expert_out,
):
    groups = lax.axis_size("expert")
    width = lax.axis_size("hidden")
    half = width // 2
    tokens_here = layer_input.shape[0]
    latent_width = latent_saved.shape[1]
    capacity = tokens_here * 3 // 32
    lanes = 128
    shard = lax.axis_index("expert")
    slot = lax.axis_index("hidden")
    ring, core = slot // 2, slot % 2

    pair_perm = [(i, i ^ 1) for i in range(width)]
    ring_groups = [[2 * i + c for i in range(half)] for c in range(2)]
    move_perm = [
        (t * width + j, (t ^ j) * width + j) for t in range(groups) for j in range(width)
    ]

    def pair_swap(x):
        m = x.shape[0] // 2
        return jnp.concatenate(
            [lax.ppermute(x[:m], "hidden", pair_perm), lax.ppermute(x[m:], "hidden", pair_perm)]
        )

    def ring_exchange(x):
        return lax.all_to_all(x, "hidden", 0, 0, tiled=True, axis_index_groups=ring_groups)

    def ring_gather(x):
        return ring_exchange(jnp.broadcast_to(x[None], (half,) + x.shape))

    def move(x):
        return lax.ppermute(x, ("expert", "hidden"), move_perm)

    steps = 2 * jnp.arange(half, dtype=jnp.int32)
    experts = shard ^ jnp.concatenate([steps + core, steps + 1 - core])
    ids_t = expert_ids.T
    member = ids_t[None] == experts[:, None, None]
    routed = jnp.any(member, axis=1)
    tri = (
        lax.broadcasted_iota(jnp.int32, (tokens_here, tokens_here), 0)
        < lax.broadcasted_iota(jnp.int32, (tokens_here, tokens_here), 1)
    ).astype(BF)
    before = mm(routed.astype(BF), tri, ((1,), (0,)))
    rank = lax.broadcasted_iota(jnp.int32, (1, capacity, 1), 1).astype(F32)
    hit = routed[:, None, :] & (before[:, None, :] == rank)
    picks = hit.astype(BF)
    rows = half * capacity
    pick_own = picks[:half].reshape(rows, tokens_here)
    pick_oth = picks[half:].reshape(rows, tokens_here)
    pick_here = lax.dynamic_index_in_dim(picks[:half], ring, 0, False)

    gate_token = jnp.sum(
        jnp.where(ids_t == (shard ^ slot), gate_values.T.astype(F32), 0.0), axis=0
    ).astype(BF)
    gate_cols = jnp.broadcast_to(gate_token[:, None], (tokens_here, lanes))
    latent_block = jnp.concatenate(
        [mm(pick_here, latent_saved, ((1,), (0,))), mm(pick_here, gate_cols, ((1,), (0,)))], axis=1
    ).astype(BF)
    latent_own = ring_gather(move(latent_block)).reshape(rows, latent_width + lanes)
    latent_oth = pair_swap(latent_own)

    def cot_part(pick):
        grads = mm(pick, output_grad, ((1,), (0,))).astype(BF)
        return mm(grads, up_proj, ((1,), (1,)))

    cot_sum = cot_part(pick_own) + pair_swap(cot_part(pick_oth).astype(BF)).astype(F32)
    cot_got = ring_exchange(cot_sum.astype(BF).reshape(half, capacity, latent_width))
    cot_block = jnp.sum(cot_got.astype(F32), axis=0).astype(BF)
    cot_own = ring_gather(move(cot_block)).reshape(rows, latent_width)
    cot_oth = pair_swap(cot_own)

    w_in = expert_in[0]
    w_out = expert_out[0]
    latent_all = jnp.concatenate([latent_own, latent_oth])
    cot_all = jnp.concatenate([cot_own, cot_oth])
    latent_rows = latent_all[:, :latent_width]
    gate_rows = latent_all[:, latent_width : latent_width + 1].astype(F32)
    act = jnp.maximum(mm(latent_rows, w_in, ((1,), (0,))), 0.0)
    back = mm(cot_all, w_out, ((1,), (1,)))
    gate_part = jnp.sum(back * act * act, axis=1, keepdims=True)
    scaled = (gate_rows * act * act).astype(BF)
    pre_grad = (2.0 * gate_rows * act * back).astype(BF)
    latent_back = mm(pre_grad, w_in, ((1,), (1,)))

    lane = lax.broadcasted_iota(jnp.int32, (1, lanes), 1)

    def pack(main, gate, hi_lane, lo_lane):
        hi = gate.astype(BF)
        lo = (gate - hi.astype(F32)).astype(BF)
        side = jnp.where(lane == hi_lane, hi, jnp.where(lane == lo_lane, lo, jnp.zeros((), BF)))
        return jnp.concatenate([main.astype(BF), side], axis=-1)

    def unpack(x):
        x = x.astype(F32)
        gate = x[..., latent_width : latent_width + 1] + x[..., latent_width + 1 : latent_width + 2]
        return x[..., :latent_width], gate

    got_main, got_gate = unpack(pair_swap(pack(latent_back[rows:], gate_part[rows:], 0, 1)))
    main = latent_back[:rows] + got_main
    gate = gate_part[:rows] + got_gate
    back_got = ring_exchange(pack(main, gate, 0, 1).reshape(half, capacity, latent_width + lanes))
    main, gate = unpack(jnp.sum(back_got.astype(F32), axis=0))
    home = move(pack(main, gate, slot, width + slot))
    home_own = ring_gather(home).reshape(rows, latent_width + lanes)
    home_oth = pair_swap(home_own)
    sums = mm(pick_own, home_own, ((0,), (0,))) + mm(pick_oth, home_oth, ((0,), (0,)))
    latent_bf = sums[:, :latent_width].astype(BF)
    by_block = (
        sums[:, latent_width : latent_width + width]
        + sums[:, latent_width + width : latent_width + 2 * width]
    )
    blocks = shard ^ jnp.arange(width, dtype=jnp.int32)
    gate_grad = jnp.sum(
        jnp.where(expert_ids[:, :, None] == blocks, by_block[:, None, :], 0.0), axis=2
    )

    input_grad = mm(latent_bf, down_proj, ((1,), (0,))).astype(BF)
    share = latent_width // groups

    def spread(a, b):
        part = mm(a, b, ((0,), (0,))).astype(BF).reshape(groups, share, b.shape[1])
        got = lax.all_to_all(part, "expert", 0, 0, tiled=True)
        return jnp.sum(got.astype(F32), axis=0)

    up_grad = spread(combined_saved, output_grad)
    down_grad = spread(latent_bf, layer_input)
    expert_out_grad = mm(scaled, cot_all, ((0,), (0,)))[None]
    expert_in_grad = mm(latent_rows, pre_grad, ((0,), (0,)))[None]
    return (input_grad, down_grad, up_grad, gate_grad, expert_in_grad, expert_out_grad)


def solution(mesh):
    return jax.shard_map(
        on_device,
        mesh=mesh,
        in_specs=(
            P("expert", "hidden"),
            P("expert", "hidden"),
            P("expert", None),
            P("expert", None),
            P("expert", None),
            P("expert", None),
            P(None, "hidden"),
            P(None, "hidden"),
            P("expert", None, "hidden"),
            P("expert", "hidden", None),
        ),
        out_specs=(
            P("expert", "hidden"),
            P("expert", "hidden"),
            P("expert", "hidden"),
            P("expert", None),
            P("expert", None, "hidden"),
            P("expert", "hidden", None),
        ),
        check_vma=False,
    )
```
